32 devices in a mesh: gx: 16 (over z, y, core), gy: 2 (over x).
Axes of the slice: x: 2, y: 2, z: 4, core: 2. Of those that a mesh axis runs over, the one named last changes fastest.
Arguments:
- spins: float32 [3, 128, 16, 256], P(None, 'gx', 'gy'), may hold values from -1 to 1, as said below
- probes: float32 [4, 8, 128, 16, 256], P(None, None, 'gx', 'gy'), may hold values from -6 to 6
- left_probes: float32 [4, 8, 128, 16, 256], P(None, None, 'gx', 'gy'), may hold values from -6 to 6
- noise: float32 [3, 128, 16, 256], P(None, 'gx', 'gy'), may hold values from -6 to 6
Outputs:
- new_spins: float32 [3, 128, 16, 256], P(None, 'gx', 'gy')
The draws below stay inside these ranges and needn't reach their ends.
Inputs may be any that keep to these rules, and one draw needn't show every extreme that they name: `spins`: every site's spin has length one.
All inputs are finite; a program needn't handle non-finite values.
Results may differ from the reference program's by a relative error of at most 0.00002.
Values sent between devices are 32-bit elements; how exact they have to be, the bound alone decides.
No kernel may reach another device: no remote copies, remote signals or barrier semaphores. Data moves between devices by JAX's collectives and lax.ppermute only.
A program may use at most 192 MiB of HBM per device.

```python
import jax
import jax.numpy as jnp
from jax import lax

NZ = 256
P_SIZE = 8
NX = 128
NY = 16


def draw_spins(key, part):
    first, second = jax.random.split(jax.random.fold_in(key, 17))
    height = jax.random.uniform(first, (NX, NY, NZ), jnp.float32, -1.0, 1.0)
    turn = jax.random.uniform(second, (NX, NY, NZ), jnp.float32, -jnp.pi, jnp.pi)
    radius = jnp.sqrt(jnp.maximum(1.0 - height * height, 0.0))
    return jnp.stack([radius * jnp.cos(turn), radius * jnp.sin(turn), height]).astype(jnp.float32)


def levels(key, shape, cuts, low, largest):
    loudness = 1.0
    for axis_at, blocks in cuts:
        draws = jax.random.uniform(jax.random.fold_in(jax.random.fold_in(key, 6), axis_at), (blocks,), jnp.float32, low / len(cuts), largest / len(cuts))
        loudness = loudness * jnp.repeat(jnp.exp(draws), shape[axis_at] // blocks).reshape((-1,) + (1,) * (len(shape) - 1 - axis_at))
    return loudness


def bell_draw(stream_key, shape, width, most, cuts=(), dtype=jnp.bfloat16):
    drawn = jax.random.normal(stream_key, shape, jnp.float32) * width
    if len(cuts) > 0:
        drawn = levels(stream_key, shape, cuts, -0.22, 0.18) * drawn
    return jnp.clip(drawn, min=-most, max=most).astype(dtype)


def setup_inputs(seed: int = 0) -> dict:
    keys = jax.random.split(jax.random.key(seed), 5)
    return {
        "spins": draw_spins(jax.random.fold_in(keys[4], 71), 0),
        "probes": bell_draw(keys[1], (4, P_SIZE, NX, NY, NZ), 1.0, 6.0, ((2, 16), (3, 2)), jnp.float32),
        "left_probes": bell_draw(keys[2], (4, P_SIZE, NX, NY, NZ), 1.0, 6.0, ((2, 16), (3, 2)), jnp.float32),
        "noise": bell_draw(keys[3], (3, NX, NY, NZ), 1.0, 6.0, ((1, 16), (2, 2)), jnp.float32),
    }


hopping = 1.0
hund_coupling = 2.0
spread = 8.5
coef_one = -1.2
coef_two = -0.8
coef_three = 0.5
time_step = 0.5
damping = 1.0
kick_scale = 0.2


def onsite(field, vector):
    spin_x, spin_y, spin_z = field[0], field[1], field[2]
    return jnp.stack([
        spin_z * vector[0] + spin_x * vector[2] + spin_y * vector[3],
        spin_z * vector[1] + spin_x * vector[3] - spin_y * vector[2],
        spin_x * vector[0] - spin_y * vector[1] - spin_z * vector[2],
        spin_x * vector[1] + spin_y * vector[0] - spin_z * vector[3]])


def bilinear(left, right):
    return jnp.stack([
        left[0] * right[2] + left[1] * right[3] + left[2] * right[0] + left[3] * right[1],
        left[0] * right[3] - left[1] * right[2] - left[2] * right[1] + left[3] * right[0],
        left[0] * right[0] + left[1] * right[1] - left[2] * right[2] - left[3] * right[3]])


def cross(first, second):
    return jnp.stack([
        first[1] * second[2] - first[2] * second[1],
        first[2] * second[0] - first[0] * second[2],
        first[0] * second[1] - first[1] * second[0]])


def hamiltonian(vector, spins):
    beside = jnp.roll(vector, 1, 1) + jnp.roll(vector, -1, 1)
    beside = beside + jnp.roll(vector, 1, 2) + jnp.roll(vector, -1, 2)
    beside = beside + jnp.roll(vector, 1, 3) + jnp.roll(vector, -1, 3)
    return (-hopping * beside - hund_coupling * onsite(spins, vector)) / spread


def reference(spins, probes, left_probes, noise):
    count = probes.shape[1]

    def one_probe(index, total):
        right = lax.dynamic_index_in_dim(probes, index, 1, keepdims=False)
        left = lax.dynamic_index_in_dim(left_probes, index, 1, keepdims=False)
        forward_one = hamiltonian(right, spins)
        forward_two = 2.0 * hamiltonian(forward_one, spins) - right
        adjoint_three = coef_three * left
        adjoint_two = coef_two * left + 2.0 * hamiltonian(adjoint_three, spins)
        adjoint_one = coef_one * left + 2.0 * hamiltonian(adjoint_two, spins) - adjoint_three
        pairs = bilinear(adjoint_one, right) + 2.0 * bilinear(adjoint_two, forward_one) + 2.0 * bilinear(adjoint_three, forward_two)
        return total + pairs

    pairs = lax.fori_loop(0, count, one_probe, jnp.zeros(spins.shape, jnp.float32))
    field = (hund_coupling / spread) / count * pairs
    torque = cross(spins, field)
    return spins - time_step * torque - time_step * damping * cross(spins, torque) + kick_scale * cross(spins, noise)
```

```python
import functools

import jax
import jax.numpy as jnp
from jax import lax
from jax.experimental import pallas as pl
from jax.experimental.pallas import tpu as pltpu
from jax.sharding import PartitionSpec as P

hopping = 1.0
hund_coupling = 2.0
spread = 8.5
coef_one = -1.2
coef_two = -0.8
coef_three = 0.5
time_step = 0.5
damping = 1.0
kick_scale = 0.2

lift = -coef_two * spread / (2.0 * coef_three)
unit = 4.0 * coef_three / (spread * spread)
tilt = -(coef_one - 3.0 * coef_three) / unit

ROWS = 8
MIB = 1 << 20
F32 = jnp.float32


def shifted(x, axis, by):
    peers = lax.axis_size(axis)
    return lax.ppermute(x, axis, [(i, (i + by) % peers) for i in range(peers)])


def bilinear(u, w):
    return [
        u[0] * w[2] + u[1] * w[3] + u[2] * w[0] + u[3] * w[1],
        u[0] * w[3] - u[1] * w[2] - u[2] * w[1] + u[3] * w[0],
        u[0] * w[0] + u[1] * w[1] - u[2] * w[2] - u[3] * w[3],
    ]


def plus(*terms):
    return [sum(parts[1:], parts[0]) for parts in zip(*terms)]


def onsite(s, v):
    return [
        s[2] * v[0] + s[0] * v[2] + s[1] * v[3],
        s[2] * v[1] + s[0] * v[3] - s[1] * v[2],
        s[0] * v[0] - s[1] * v[1] - s[2] * v[2],
        s[0] * v[1] + s[1] * v[0] - s[2] * v[3],
    ]


def row_index(like):
    return lax.broadcasted_iota(jnp.int32, like.shape, 0)


def along(v):
    rows = row_index(v)
    lanes = v.shape[1]
    down = jnp.where(rows == 0, 0.0, pltpu.roll(v, 1, 0))
    up = jnp.where(rows == ROWS - 1, 0.0, pltpu.roll(v, ROWS - 1, 0))
    return down + up + pltpu.roll(v, 1, 1) + pltpu.roll(v, lanes - 1, 1)


def doubled(spin_ref, rows):
    return [hund_coupling * spin_ref[i, rows, :] for i in range(3)]


def pack_kernel(p_ref, l_ref, ysend_ref):
    wide = p_ref.shape[1] // ROWS
    for k, ref in enumerate((p_ref, l_ref)):
        for c in range(4):
            ysend_ref[0, k, c] = ref[c, pl.ds(0, wide, stride=ROWS), :]
            ysend_ref[1, k, c] = ref[c, pl.ds(ROWS - 1, wide, stride=ROWS), :]


def rest_kernel(p_ref, l_ref, s_ref, yin_ref, sy_ref):
    wide = p_ref.shape[1] // ROWS
    for k, ref in enumerate((p_ref, l_ref)):
        for c in range(4):
            yin_ref[0, k, c] = ref[c, pl.ds(1, wide, stride=ROWS), :]
            yin_ref[1, k, c] = ref[c, pl.ds(ROWS - 2, wide, stride=ROWS), :]
    for i in range(3):
        sy_ref[0, i] = s_ref[i, pl.ds(0, wide, stride=ROWS), :]
        sy_ref[1, i] = s_ref[i, pl.ds(ROWS - 1, wide, stride=ROWS), :]


def inner_kernel(p_ref, l_ref, s_ref, g_ref, fx_ref, fy_ref, f_ref, a_ref):
    wide = p_ref.shape[1] // ROWS
    half = f_ref.shape[3]

    @pl.when(pl.program_id(0) == 0)
    def _():
        g_ref[...] = jnp.zeros_like(g_ref)

    def at(x):
        return slice(x * ROWS, (x + 1) * ROWS)

    def plain(ref):
        return lambda c, x: ref[c, at(x), :]

    def joined(ref):
        return lambda c, x: jnp.concatenate([ref[c, 0, at(x), :], ref[c, 1, at(x), :]], 1)

    def neighbours(load, c, x, centre):
        total = along(centre)
        if x > 0:
            total = total + load(c, x - 1)
        if x < wide - 1:
            total = total + load(c, x + 1)
        return total

    load_p, load_l, load_f, load_a = plain(p_ref), plain(l_ref), joined(f_ref), joined(a_ref)
    for x in range(wide):
        spin = doubled(s_ref, at(x))
        for load, dst, extra in ((load_p, f_ref, 0.0), (load_l, a_ref, lift)):
            v = [load(c, x) for c in range(4)]
            m = onsite(spin, v)
            for c in range(4):
                out = neighbours(load, c, x, v[c]) + m[c]
                if extra:
                    out = out + extra * v[c]
                dst[c, 0, at(x), :] = out[:, :half]
                dst[c, 1, at(x), :] = out[:, half:]
    for x in range(wide):
        spin = doubled(s_ref, at(x))
        p, l, f, a = ([load(c, x) for c in range(4)] for load in (load_p, load_l, load_f, load_a))
        ma, mf = onsite(spin, a), onsite(spin, f)
        ha = [neighbours(load_a, c, x, a[c]) + ma[c] - tilt * l[c] for c in range(4)]
        hf = [neighbours(load_f, c, x, f[c]) + mf[c] for c in range(4)]
        total = plus(bilinear(ha, p), bilinear(a, f), bilinear(l, hf))
        for i in range(3):
            g_ref[i, at(x), :] += total[i]
    for k, ref in enumerate((f_ref, a_ref)):
        for c in range(4):
            for z in range(2):
                lanes = slice(z * half, (z + 1) * half)
                fx_ref[0, k, c, :, lanes] = ref[c, z, at(0), :]
                fx_ref[1, k, c, :, lanes] = ref[c, z, at(wide - 1), :]
                fy_ref[0, k, c, :, lanes] = ref[c, z, pl.ds(0, wide, stride=ROWS), :]
                fy_ref[1, k, c, :, lanes] = ref[c, z, pl.ds(ROWS - 1, wide, stride=ROWS), :]


def own_change(spin, p, l, p_in, l_in, f, a, dp, dl):
    hp = plus(onsite(spin, dp), [along(v) for v in dp])
    hl = plus(onsite(spin, dl), [along(v) for v in dl])
    here = plus(
        bilinear(dl, plus(f, dp)), bilinear(a, dp), bilinear(hl, p), bilinear(l, hp)
    )
    inward = plus(bilinear(dl, p_in), bilinear(l_in, dp))
    return here, inward


def corner_rows(lo_ref, hi_ref, k, c, row, wide, lanes):
    rows = lax.broadcasted_iota(jnp.int32, (wide, lanes), 0)
    low = jnp.broadcast_to(lo_ref[k, c, row : row + 1, :], (wide, lanes))
    high = jnp.broadcast_to(hi_ref[k, c, row : row + 1, :], (wide, lanes))
    return jnp.where(rows == 0, low, jnp.where(rows == wide - 1, high, 0.0))


def x_kernel(
    p_ref, l_ref, s_ref, fx_ref, fy_ref, lo_ref, hi_ref, mlo_ref, mhi_ref, gx_ref, fe_ref
):
    wide = p_ref.shape[1] // ROWS
    lanes = p_ref.shape[2]

    @pl.when(pl.program_id(0) == 0)
    def _():
        mlo_ref[...] = jnp.zeros_like(mlo_ref)
        mhi_ref[...] = jnp.zeros_like(mhi_ref)
        gx_ref[...] = jnp.zeros_like(gx_ref)

    sides = ((0, lo_ref, mlo_ref, 0, 1), (1, hi_ref, mhi_ref, wide - 1, wide - 2))
    for side, halo_ref, m_ref, x, x_in in sides:
        rows = slice(x * ROWS, (x + 1) * ROWS)
        rows_in = slice(x_in * ROWS, (x_in + 1) * ROWS)
        spin = doubled(s_ref, rows)
        p, p_in = ([p_ref[c, r, :] for c in range(4)] for r in (rows, rows_in))
        l, l_in = ([l_ref[c, r, :] for c in range(4)] for r in (rows, rows_in))
        f = [fx_ref[side, 0, c] for c in range(4)]
        a = [fx_ref[side, 1, c] for c in range(4)]
        dp = [halo_ref[0, c] for c in range(4)]
        dl = [halo_ref[1, c] for c in range(4)]
        message = plus(bilinear(plus(a, dl), dp), bilinear(dl, plus(f, dp)))
        here, inward = own_change(spin, p, l, p_in, l_in, f, a, dp, dl)
        for i in range(3):
            m_ref[i] += message[i]
            gx_ref[side, 0, i] += here[i]
            gx_ref[side, 1, i] += inward[i]
    for side, row in ((0, 0), (1, ROWS - 1)):
        for k in range(2):
            for c in range(4):
                t = corner_rows(lo_ref, hi_ref, k, c, row, wide, lanes)
                fe_ref[side, k, c] = fy_ref[side, k, c] + 2.0 * t


def y_message_kernel(recv_ref, fe_ref, my_ref):
    probes = fe_ref.shape[3]
    for side in range(2):

        def body(q, total):
            dp = [recv_ref[1 - side, 0, c, q] for c in range(4)]
            dl = [recv_ref[1 - side, 1, c, q] for c in range(4)]
            f = [fe_ref[side, 0, c, q] for c in range(4)]
            a = [fe_ref[side, 1, c, q] for c in range(4)]
            return tuple(
                plus(total, bilinear(plus(a, dl), dp), bilinear(dl, plus(f, dp)))
            )

        zero = jnp.zeros(my_ref.shape[2:], F32)
        total = lax.fori_loop(0, probes, body, (zero, zero, zero), unroll=2)
        for i in range(3):
            my_ref[side, i] = total[i]


def y_kernel(recv_ref, ysend_ref, yin_ref, fy_ref, lo_ref, hi_ref, sy_ref, gy_ref):
    probes = fy_ref.shape[3]
    wide, lanes = fy_ref.shape[4:]
    for side, row in ((0, 0), (1, ROWS - 1)):
        spin = [hund_coupling * sy_ref[side, i] for i in range(3)]

        def body(q, total):
            dp = [recv_ref[1 - side, 0, c, q] for c in range(4)]
            dl = [recv_ref[1 - side, 1, c, q] for c in range(4)]
            lo, hi = lo_ref.at[:, :, q], hi_ref.at[:, :, q]
            f, a = (
                [
                    fy_ref[side, k, c, q]
                    + corner_rows(lo, hi, k, c, row, wide, lanes)
                    for c in range(4)
                ]
                for k in range(2)
            )
            p, l = ([ysend_ref[side, k, c, q] for c in range(4)] for k in range(2))
            p_in, l_in = ([yin_ref[side, k, c, q] for c in range(4)] for k in range(2))
            here, inward = own_change(spin, p, l, p_in, l_in, f, a, dp, dl)
            return tuple(plus(total, here + inward))

        zero = jnp.zeros((wide, lanes), F32)
        total = lax.fori_loop(0, probes, body, (zero,) * 6)
        for j in range(2):
            for i in range(3):
                gy_ref[side, j, i] = total[3 * j + i]


def cross(a, b):
    return [
        a[1] * b[2] - a[2] * b[1],
        a[2] * b[0] - a[0] * b[2],
        a[0] * b[1] - a[1] * b[0],
    ]


def final_kernel(scale, g_ref, gx_ref, mlo_ref, mhi_ref, gy_ref, my_ref, s_ref, n_ref, o_ref):
    wide, lanes = gy_ref.shape[3:]
    rows = lax.broadcasted_iota(jnp.int32, (ROWS, lanes), 0)
    for x in range(wide):
        here = slice(x * ROWS, (x + 1) * ROWS)
        field = []
        for i in range(3):
            g = g_ref[i, here, :]
            for side, edge, step, m_ref in ((0, 0, 1, mlo_ref), (1, wide - 1, -1, mhi_ref)):
                if x == edge:
                    g = g + gx_ref[side, 0, i] + m_ref[i]
                if x == edge + step:
                    g = g + gx_ref[side, 1, i]
            for side, edge, step in ((0, 0, 1), (1, ROWS - 1, -1)):
                at = slice(x, x + 1)
                outer = gy_ref[side, 0, i, at, :] + my_ref[1 - side, i, at, :]
                inner = gy_ref[side, 1, i, at, :]
                outer = jnp.broadcast_to(outer, (ROWS, lanes))
                inner = jnp.broadcast_to(inner, (ROWS, lanes))
                g = g + jnp.where(
                    rows == edge, outer, jnp.where(rows == edge + step, inner, 0.0)
                )
            field.append(scale * g)
        s = [s_ref[i, here, :] for i in range(3)]
        kick = [n_ref[i, here, :] for i in range(3)]
        torque = cross(s, field)
        twist = cross(s, torque)
        kick = cross(s, kick)
        for i in range(3):
            o_ref[i, here, :] = (
                s[i]
                - time_step * torque[i]
                - time_step * damping * twist[i]
                + kick_scale * kick[i]
            )


def call(kernel, name, out_shape, flops, moved, **kw):
    limit = kw.pop("limit", 16)
    return pl.pallas_call(
        kernel,
        out_shape=[jax.ShapeDtypeStruct(s, F32) for s in out_shape],
        compiler_params=pltpu.CompilerParams(vmem_limit_bytes=limit * MIB),
        cost_estimate=pl.CostEstimate(flops=flops, bytes_accessed=moved, transcendentals=0),
        name=name,
        **kw,
    )


def local(spins, probes, left_probes, noise):
    _, count, wide, tall, deep = probes.shape
    assert tall == ROWS and wide == ROWS
    sites = wide * tall
    p = probes.reshape(4, count, sites, deep)
    l = left_probes.reshape(4, count, sites, deep)
    s = spins.reshape(3, sites, deep)
    n = noise.reshape(3, sites, deep)
    volume = 4 * count * sites * deep
    plane = (4, count, ROWS, deep)

    def by_probe(lead):
        ones = (0,) * len(lead)
        return pl.BlockSpec(
            lead + (4, None, ROWS, deep), lambda q: ones + (0, q, 0, 0)
        )

    def whole(shape):
        return pl.BlockSpec(shape, lambda q: (0,) * len(shape))

    field_block = pl.BlockSpec((4, None, sites, deep), lambda q: (0, q, 0, 0))
    vmem = pl.BlockSpec(memory_space=pltpu.VMEM)

    def half_block(lead):
        zero = (0,) * len(lead)
        return pl.BlockSpec(lead + (4, None, ROWS, deep // 2), lambda q, z: zero + (0, q, 0, z))

    half_field = pl.BlockSpec((4, None, sites, deep // 2), lambda q, z: (0, q, 0, z))
    (ysend,) = call(
        pack_kernel, "pack", [(2, 2) + plane], volume, 8 * volume,
        grid=(count, 2),
        in_specs=[half_field, half_field],
        out_specs=[half_block((2, 2))],
    )(p, l)

    def meet(pair):
        if lax.axis_size("gy") == 2:
            return shifted(pair, "gy", 1)
        return jnp.stack([shifted(pair[0], "gy", -1), shifted(pair[1], "gy", 1)])

    recv = meet(ysend)
    hi = shifted(jnp.stack([p[:, :, :ROWS], l[:, :, :ROWS]]), "gx", -1)
    lo = shifted(jnp.stack([p[:, :, sites - ROWS :], l[:, :, sites - ROWS :]]), "gx", 1)

    yin, sy = call(
        rest_kernel, "rest", [(2, 2) + plane, (2, 3, wide, deep)], volume, 8 * volume,
        grid=(2, count),
        in_specs=[
            pl.BlockSpec((4, None, sites, deep // 2), lambda z, q: (0, q, 0, z)),
            pl.BlockSpec((4, None, sites, deep // 2), lambda z, q: (0, q, 0, z)),
            pl.BlockSpec((3, sites, deep // 2), lambda z, q: (0, 0, z)),
        ],
        out_specs=[
            pl.BlockSpec((2, 2, 4, None, wide, deep // 2), lambda z, q: (0, 0, 0, q, 0, z)),
            pl.BlockSpec((2, 3, wide, deep // 2), lambda z, q: (0, 0, 0, z)),
        ],
    )(p, l, s)

    g, fx, fy = call(
        inner_kernel, "inner", [(3, sites, deep)] + [(2, 2) + plane] * 2,
        80 * volume, 16 * volume,
        grid=(count,),
        in_specs=[field_block, field_block, whole((3, sites, deep))],
        out_specs=[whole((3, sites, deep))] + [by_probe((2, 2))] * 2,
        scratch_shapes=[pltpu.VMEM((4, 2, sites, deep // 2), F32)] * 2,
    )(p, l, s)

    mlo, mhi, gx, fe = call(
        x_kernel, "edges_x",
        [(3, ROWS, deep)] * 2 + [(2, 2, 3, ROWS, deep), (2, 2) + plane],
        20 * volume, 16 * volume,
        grid=(count,),
        in_specs=[field_block, field_block, whole((3, sites, deep))]
        + [by_probe((2, 2))] * 2 + [by_probe((2,))] * 2,
        out_specs=[whole((3, ROWS, deep))] * 2
        + [whole((2, 2, 3, ROWS, deep)), by_probe((2, 2))],
    )(p, l, s, fx, fy, lo, hi)
    mhi_recv = shifted(mlo, "gx", -1)
    mlo_recv = shifted(mhi, "gx", 1)

    (my,) = call(
        y_message_kernel, "message_y", [(2, 3, wide, deep)], 5 * volume, 4 * volume,
        in_specs=[vmem] * 2, out_specs=[vmem],
    )(recv, fe)
    my_recv = meet(my)

    (gy,) = call(
        y_kernel, "edges_y", [(2, 2, 3, wide, deep)], 20 * volume, 8 * volume,
        in_specs=[vmem] * 7, out_specs=[vmem],
    )(recv, ysend, yin, fy, lo, hi, sy)

    (out,) = call(
        functools.partial(final_kernel, hund_coupling / spread / count * unit),
        "final", [(3, sites, deep)], volume, volume,
        in_specs=[vmem] * 8, out_specs=[vmem],
    )(g, gx, mlo_recv, mhi_recv, gy, my_recv, s, n)
    return out.reshape(spins.shape)


def solution(mesh):
    placed = (
        P(None, "gx", "gy", None),
        P(None, None, "gx", "gy", None),
        P(None, None, "gx", "gy", None),
        P(None, "gx", "gy", None),
    )
    return jax.shard_map(
        local, mesh=mesh, in_specs=placed, out_specs=P(None, "gx", "gy", None), check_vma=False
    )
```

```python
import functools

import jax
import jax.numpy as jnp
from jax import lax
from jax.experimental import pallas as pl
from jax.experimental.pallas import tpu as pltpu
from jax.sharding import PartitionSpec as P

hopping = 1.0
hund_coupling = 2.0
spread = 8.5
coef_one = -1.2
coef_two = -0.8
coef_three = 0.5
time_step = 0.5
damping = 1.0
kick_scale = 0.2

lift = -coef_two * spread / (2.0 * coef_three)
unit = 4.0 * coef_three / (spread * spread)
tilt = -(coef_one - 3.0 * coef_three) / unit

ROWS = 8
MIB = 1 << 20
F32 = jnp.float32


def shifted(x, axis, by):
    peers = lax.axis_size(axis)
    return lax.ppermute(x, axis, [(i, (i + by) % peers) for i in range(peers)])


def bilinear(u, w):
    return [
        u[0] * w[2] + u[1] * w[3] + u[2] * w[0] + u[3] * w[1],
        u[0] * w[3] - u[1] * w[2] - u[2] * w[1] + u[3] * w[0],
        u[0] * w[0] + u[1] * w[1] - u[2] * w[2] - u[3] * w[3],
    ]


def plus(*terms):
    return [sum(parts[1:], parts[0]) for parts in zip(*terms)]


def onsite(s, v):
    return [
        s[2] * v[0] + s[0] * v[2] + s[1] * v[3],
        s[2] * v[1] + s[0] * v[3] - s[1] * v[2],
        s[0] * v[0] - s[1] * v[1] - s[2] * v[2],
        s[0] * v[1] + s[1] * v[0] - s[2] * v[3],
    ]


def row_index(like):
    return lax.broadcasted_iota(jnp.int32, like.shape, 0)


def along(v):
    rows = row_index(v)
    lanes = v.shape[1]
    down = jnp.where(rows == 0, 0.0, pltpu.roll(v, 1, 0))
    up = jnp.where(rows == ROWS - 1, 0.0, pltpu.roll(v, ROWS - 1, 0))
    return down + up + pltpu.roll(v, 1, 1) + pltpu.roll(v, lanes - 1, 1)


def doubled(spin_ref, rows):
    return [hund_coupling * spin_ref[i, rows, :] for i in range(3)]


def copy_all(copies):
    for copy in copies:
        copy.start()
    for copy in copies:
        copy.wait()


def y_rows(refs, rows, out, sems, first):
    return [
        pltpu.make_async_copy(
            ref.at[:, :, :, row, :], out.at[j, k], sems.at[first + 2 * j + k]
        )
        for j, row in enumerate(rows)
        for k, ref in enumerate(refs)
    ]


def x_planes(refs, planes, outs, sems, first):
    return [
        pltpu.make_async_copy(
            ref.at[:, :, plane, :, :], out.at[k], sems.at[first + 2 * j + k]
        )
        for j, (plane, out) in enumerate(zip(planes, outs))
        for k, ref in enumerate(refs)
    ]


def pack_y_kernel(p_ref, l_ref, ysend_ref, sems):
    copy_all(y_rows((p_ref, l_ref), (0, ROWS - 1), ysend_ref, sems, 0))


def pack_x_kernel(p_ref, l_ref, xlo_ref, xhi_ref, sems):
    wide = p_ref.shape[2]
    copy_all(x_planes((p_ref, l_ref), (0, wide - 1), (xlo_ref, xhi_ref), sems, 0))


def inner_kernel(
    p_ref, l_ref, s_ref, p_hbm, l_hbm, s_hbm,
    g_ref, fx_ref, fy_ref, xin_ref, yin_ref, sy_ref, f_ref, a_ref, sems,
):
    wide = p_ref.shape[1] // ROWS
    half = f_ref.shape[3]
    copies = x_planes((p_hbm, l_hbm), (1, wide - 2), (xin_ref.at[0], xin_ref.at[1]), sems, 0)
    copies += y_rows((p_hbm, l_hbm), (1, ROWS - 2), yin_ref, sems, 4)
    copies += [
        pltpu.make_async_copy(s_hbm.at[:, :, row, :], sy_ref.at[j], sems.at[8 + j])
        for j, row in enumerate((0, ROWS - 1))
    ]

    @pl.when(pl.program_id(0) == 0)
    def _():
        for copy in copies:
            copy.start()
        g_ref[...] = jnp.zeros_like(g_ref)

    @pl.when(pl.program_id(0) == pl.num_programs(0) - 1)
    def _():
        for copy in copies:
            copy.wait()

    def at(x):
        return slice(x * ROWS, (x + 1) * ROWS)

    def plain(ref):
        return lambda c, x: ref[c, at(x), :]

    def joined(ref):
        return lambda c, x: jnp.concatenate([ref[c, 0, at(x), :], ref[c, 1, at(x), :]], 1)

    def neighbours(load, c, x, centre):
        total = along(centre)
        if x > 0:
            total = total + load(c, x - 1)
        if x < wide - 1:
            total = total + load(c, x + 1)
        return total

    load_p, load_l, load_f, load_a = plain(p_ref), plain(l_ref), joined(f_ref), joined(a_ref)
    for x in range(wide):
        spin = doubled(s_ref, at(x))
        for load, dst, extra in ((load_p, f_ref, 0.0), (load_l, a_ref, lift)):
            v = [load(c, x) for c in range(4)]
            m = onsite(spin, v)
            for c in range(4):
                out = neighbours(load, c, x, v[c]) + m[c]
                if extra:
                    out = out + extra * v[c]
                dst[c, 0, at(x), :] = out[:, :half]
                dst[c, 1, at(x), :] = out[:, half:]
    for x in range(wide):
        spin = doubled(s_ref, at(x))
        p, l, f, a = ([load(c, x) for c in range(4)] for load in (load_p, load_l, load_f, load_a))
        ma, mf = onsite(spin, a), onsite(spin, f)
        ha = [neighbours(load_a, c, x, a[c]) + ma[c] - tilt * l[c] for c in range(4)]
        hf = [neighbours(load_f, c, x, f[c]) + mf[c] for c in range(4)]
        total = plus(bilinear(ha, p), bilinear(a, f), bilinear(l, hf))
        for i in range(3):
            g_ref[i, at(x), :] += total[i]
    for k, ref in enumerate((f_ref, a_ref)):
        for c in range(4):
            for z in range(2):
                lanes = slice(z * half, (z + 1) * half)
                fx_ref[0, k, c, :, lanes] = ref[c, z, at(0), :]
                fx_ref[1, k, c, :, lanes] = ref[c, z, at(wide - 1), :]
                fy_ref[0, k, c, :, lanes] = ref[c, z, pl.ds(0, wide, stride=ROWS), :]
                fy_ref[1, k, c, :, lanes] = ref[c, z, pl.ds(ROWS - 1, wide, stride=ROWS), :]


def own_change(spin, p, l, p_in, l_in, f, a, dp, dl):
    hp = plus(onsite(spin, dp), [along(v) for v in dp])
    hl = plus(onsite(spin, dl), [along(v) for v in dl])
    here = plus(
        bilinear(dl, plus(f, dp)), bilinear(a, dp), bilinear(hl, p), bilinear(l, hp)
    )
    inward = plus(bilinear(dl, p_in), bilinear(l_in, dp))
    return here, inward


def corner_rows(lo_ref, hi_ref, k, c, row, wide, lanes):
    rows = lax.broadcasted_iota(jnp.int32, (wide, lanes), 0)
    low = jnp.broadcast_to(lo_ref[k, c, row : row + 1, :], (wide, lanes))
    high = jnp.broadcast_to(hi_ref[k, c, row : row + 1, :], (wide, lanes))
    return jnp.where(rows == 0, low, jnp.where(rows == wide - 1, high, 0.0))


def over_probes(probes, body, results, like, unroll):
    zero = jnp.zeros(like, F32)
    return lax.fori_loop(0, probes, body, (zero,) * results, unroll=unroll)


def spinors(ref, k, q):
    return [ref[k, c, q] for c in range(4)]


def message(f, a, dp, dl):
    return plus(bilinear(plus(a, dl), dp), bilinear(dl, plus(f, dp)))


def x_message_kernel(fx_ref, lo_ref, hi_ref, mlo_ref, mhi_ref):
    probes = fx_ref.shape[3]
    for side, halo, out in ((0, lo_ref, mlo_ref), (1, hi_ref, mhi_ref)):

        def body(q, total):
            f, a = (spinors(fx_ref.at[side], k, q) for k in range(2))
            dp, dl = (spinors(halo, k, q) for k in range(2))
            return tuple(plus(total, message(f, a, dp, dl)))

        total = over_probes(probes, body, 3, out.shape[1:], 2)
        for i in range(3):
            out[i] = total[i]


def x_kernel(
    fx_ref, fy_ref, lo_ref, hi_ref, xlo_ref, xhi_ref, xin_ref, s_ref, gx_ref, fe_ref
):
    probes = fx_ref.shape[3]
    wide, lanes = fy_ref.shape[4:]
    for side, halo, edge, x in ((0, lo_ref, xlo_ref, 0), (1, hi_ref, xhi_ref, wide - 1)):
        spin = doubled(s_ref, slice(x * ROWS, (x + 1) * ROWS))

        def body(q, total):
            f, a = (spinors(fx_ref.at[side], k, q) for k in range(2))
            dp, dl = (spinors(halo, k, q) for k in range(2))
            p, l = (spinors(edge, k, q) for k in range(2))
            p_in, l_in = (spinors(xin_ref.at[side], k, q) for k in range(2))
            here, inward = own_change(spin, p, l, p_in, l_in, f, a, dp, dl)
            row = side * (ROWS - 1)
            for k in range(2):
                for c in range(4):
                    t = corner_rows(lo_ref.at[:, :, q], hi_ref.at[:, :, q], k, c, row, wide, lanes)
                    fe_ref[side, k, c, q] = fy_ref[side, k, c, q] + 2.0 * t
            return tuple(plus(total, here + inward))

        total = over_probes(probes, body, 6, (ROWS, lanes), 1)
        for j in range(2):
            for i in range(3):
                gx_ref[side, j, i] = total[3 * j + i]


def y_message_kernel(recv_ref, fe_ref, base_ref, my_ref):
    probes = fe_ref.shape[3]
    for side in range(2):

        def body(q, total):
            f, a = (spinors(fe_ref.at[side], k, q) for k in range(2))
            dp, dl = (spinors(recv_ref.at[1 - side], k, q) for k in range(2))
            return tuple(plus(total, message(f, a, dp, dl)))

        total = over_probes(probes, body, 3, my_ref.shape[2:], 2)
        for i in range(3):
            my_ref[side, i] = total[i]


def y_kernel(recv_ref, ysend_ref, yin_ref, fy_ref, lo_ref, hi_ref, sy_ref, gy_ref):
    probes = fy_ref.shape[3]
    wide, lanes = fy_ref.shape[4:]
    for side, row in ((0, 0), (1, ROWS - 1)):
        spin = [hund_coupling * sy_ref[side, i] for i in range(3)]

        def body(q, total):
            dp, dl = (spinors(recv_ref.at[1 - side], k, q) for k in range(2))
            lo, hi = lo_ref.at[:, :, q], hi_ref.at[:, :, q]
            f, a = (
                [
                    fy_ref[side, k, c, q]
                    + corner_rows(lo, hi, k, c, row, wide, lanes)
                    for c in range(4)
                ]
                for k in range(2)
            )
            p, l = (spinors(ysend_ref.at[side], k, q) for k in range(2))
            p_in, l_in = (spinors(yin_ref.at[side], k, q) for k in range(2))
            here, inward = own_change(spin, p, l, p_in, l_in, f, a, dp, dl)
            return tuple(plus(total, here + inward))

        total = over_probes(probes, body, 6, (wide, lanes), 1)
        for j in range(2):
            for i in range(3):
                gy_ref[side, j, i] = total[3 * j + i]


def cross(a, b):
    return [
        a[1] * b[2] - a[2] * b[1],
        a[2] * b[0] - a[0] * b[2],
        a[0] * b[1] - a[1] * b[0],
    ]


def base_kernel(g_ref, gx_ref, mlo_ref, mhi_ref, base_ref):
    sites = g_ref.shape[1]
    wide = sites // ROWS
    base_ref[...] = g_ref[...]
    for side, x, step, m_ref in ((0, 0, 1, mlo_ref), (1, wide - 1, -1, mhi_ref)):
        for i in range(3):
            here = slice(x * ROWS, (x + 1) * ROWS)
            inward = slice((x + step) * ROWS, (x + step + 1) * ROWS)
            base_ref[i, here, :] += gx_ref[side, 0, i] + m_ref[i]
            base_ref[i, inward, :] += gx_ref[side, 1, i]


def final_kernel(scale, g_ref, gy_ref, my_ref, s_ref, n_ref, o_ref):
    wide, lanes = gy_ref.shape[3:]
    rows = lax.broadcasted_iota(jnp.int32, (ROWS, lanes), 0)
    for x in range(wide):
        here = slice(x * ROWS, (x + 1) * ROWS)
        field = []
        for i in range(3):
            g = g_ref[i, here, :]
            for side, edge, step in ((0, 0, 1), (1, ROWS - 1, -1)):
                at = slice(x, x + 1)
                outer = gy_ref[side, 0, i, at, :] + my_ref[1 - side, i, at, :]
                inner = gy_ref[side, 1, i, at, :]
                outer = jnp.broadcast_to(outer, (ROWS, lanes))
                inner = jnp.broadcast_to(inner, (ROWS, lanes))
                g = g + jnp.where(
                    rows == edge, outer, jnp.where(rows == edge + step, inner, 0.0)
                )
            field.append(scale * g)
        s = [s_ref[i, here, :] for i in range(3)]
        kick = [n_ref[i, here, :] for i in range(3)]
        torque = cross(s, field)
        twist = cross(s, torque)
        kick = cross(s, kick)
        for i in range(3):
            o_ref[i, here, :] = (
                s[i]
                - time_step * torque[i]
                - time_step * damping * twist[i]
                + kick_scale * kick[i]
            )


def call(kernel, name, out_shape, flops, moved, **kw):
    limit = kw.pop("limit", 16)
    return pl.pallas_call(
        kernel,
        out_shape=[jax.ShapeDtypeStruct(s, F32) for s in out_shape],
        compiler_params=pltpu.CompilerParams(vmem_limit_bytes=limit * MIB),
        cost_estimate=pl.CostEstimate(flops=flops, bytes_accessed=moved, transcendentals=0),
        name=name,
        **kw,
    )


def local(spins, probes, left_probes, noise):
    _, count, wide, tall, deep = probes.shape
    assert tall == ROWS and wide == ROWS
    sites = wide * tall
    flat = (4, count, sites, deep)
    p5, l5, s4, p, l = (
        pltpu.with_memory_space_constraint(v, pltpu.HBM)
        for v in (probes, left_probes, spins, probes.reshape(flat), left_probes.reshape(flat))
    )
    s, n = spins.reshape(3, sites, deep), noise.reshape(3, sites, deep)
    volume = 4 * count * sites * deep
    plane = (4, count, ROWS, deep)
    pair = (2, 2) + plane
    vmem = pl.BlockSpec(memory_space=pltpu.VMEM)
    hbm = pl.BlockSpec(memory_space=pltpu.HBM)

    def meet(both):
        if lax.axis_size("gy") == 2:
            return shifted(both, "gy", 1)
        return jnp.stack([shifted(both[0], "gy", -1), shifted(both[1], "gy", 1)])

    (ysend,) = call(
        pack_y_kernel, "pack_y", [pair], volume, 2 * volume,
        in_specs=[hbm] * 2, out_specs=[vmem],
        scratch_shapes=[pltpu.SemaphoreType.DMA((4,))],
    )(p5, l5)
    recv = meet(ysend)
    xlo, xhi = call(
        pack_x_kernel, "pack_x", [(2,) + plane] * 2, volume, 2 * volume,
        in_specs=[hbm] * 2, out_specs=[vmem] * 2,
        scratch_shapes=[pltpu.SemaphoreType.DMA((4,))],
    )(p5, l5)
    hi = shifted(xlo, "gx", -1)
    lo = shifted(xhi, "gx", 1)

    def by_probe():
        return pl.BlockSpec((2, 2, 4, None, ROWS, deep), lambda q: (0, 0, 0, q, 0, 0))

    def whole(shape):
        return pl.BlockSpec(shape, lambda q: (0,) * len(shape))

    field_block = pl.BlockSpec((4, None, sites, deep), lambda q: (0, q, 0, 0))
    g, fx, fy, xin, yin, sy = call(
        inner_kernel, "inner",
        [(3, sites, deep)] + [pair] * 4 + [(2, 3, wide, deep)],
        80 * volume, 16 * volume,
        grid=(count,),
        in_specs=[field_block, field_block, whole((3, sites, deep))] + [hbm] * 3,
        out_specs=[whole((3, sites, deep))] + [by_probe()] * 2 + [vmem] * 3,
        scratch_shapes=[pltpu.VMEM((4, 2, sites, deep // 2), F32)] * 2
        + [pltpu.SemaphoreType.DMA((10,))],
    )(p, l, s, p5, l5, s4)

    mlo, mhi = call(
        x_message_kernel, "message_x", [(3, ROWS, deep)] * 2, 5 * volume, 4 * volume,
        in_specs=[vmem] * 3, out_specs=[vmem] * 2,
    )(fx, lo, hi)
    mhi_recv = shifted(mlo, "gx", -1)
    mlo_recv = shifted(mhi, "gx", 1)
    gx, fe = call(
        x_kernel, "edges_x", [(2, 2, 3, ROWS, deep), pair], 20 * volume, 8 * volume,
        in_specs=[vmem] * 8, out_specs=[vmem] * 2,
    )(fx, fy, lo, hi, xlo, xhi, xin, s)
    (base,) = call(
        base_kernel, "base", [(3, sites, deep)], volume, volume,
        in_specs=[vmem] * 4, out_specs=[vmem],
    )(g, gx, mlo_recv, mhi_recv)

    (my,) = call(
        y_message_kernel, "message_y", [(2, 3, wide, deep)], 5 * volume, 4 * volume,
        in_specs=[vmem] * 2 + [pl.BlockSpec(memory_space=pl.ANY)], out_specs=[vmem],
    )(recv, fe, base)
    my_recv = meet(my)
    (gy,) = call(
        y_kernel, "edges_y", [(2, 2, 3, wide, deep)], 20 * volume, 8 * volume,
        in_specs=[vmem] * 7, out_specs=[vmem],
    )(recv, ysend, yin, fy, lo, hi, sy)

    (out,) = call(
        functools.partial(final_kernel, hund_coupling / spread / count * unit),
        "final", [(3, sites, deep)], volume, volume,
        in_specs=[vmem] * 5, out_specs=[vmem],
    )(base, gy, my_recv, s, n)
    return out.reshape(spins.shape)


def solution(mesh):
    placed = (
        P(None, "gx", "gy", None),
        P(None, None, "gx", "gy", None),
        P(None, None, "gx", "gy", None),
        P(None, "gx", "gy", None),
    )
    return jax.shard_map(
        local, mesh=mesh, in_specs=placed, out_specs=P(None, "gx", "gy", None), check_vma=False
    )
```

```python
import functools

import jax
import jax.numpy as jnp
from jax import lax
from jax.experimental import pallas as pl
from jax.experimental.pallas import tpu as pltpu
from jax.sharding import PartitionSpec as P

hopping = 1.0
hund_coupling = 2.0
spread = 8.5
coef_one = -1.2
coef_two = -0.8
coef_three = 0.5
time_step = 0.5
damping = 1.0
kick_scale = 0.2

lift = -coef_two * spread / (2.0 * coef_three)
unit = 4.0 * coef_three / (spread * spread)
tilt = -(coef_one - 3.0 * coef_three) / unit

ROWS = 8
MIB = 1 << 20
F32 = jnp.float32


def shifted(x, axis, by):
    peers = lax.axis_size(axis)
    return lax.ppermute(x, axis, [(i, (i + by) % peers) for i in range(peers)])


def bilinear(u, w):
    return [
        u[0] * w[2] + u[1] * w[3] + u[2] * w[0] + u[3] * w[1],
        u[0] * w[3] - u[1] * w[2] - u[2] * w[1] + u[3] * w[0],
        u[0] * w[0] + u[1] * w[1] - u[2] * w[2] - u[3] * w[3],
    ]


def plus(*terms):
    return [sum(parts[1:], parts[0]) for parts in zip(*terms)]


def onsite(s, v):
    return [
        s[2] * v[0] + s[0] * v[2] + s[1] * v[3],
        s[2] * v[1] + s[0] * v[3] - s[1] * v[2],
        s[0] * v[0] - s[1] * v[1] - s[2] * v[2],
        s[0] * v[1] + s[1] * v[0] - s[2] * v[3],
    ]


def row_index(like):
    return lax.broadcasted_iota(jnp.int32, like.shape, 0)


def along(v):
    rows = row_index(v)
    lanes = v.shape[1]
    down = jnp.where(rows == 0, 0.0, pltpu.roll(v, 1, 0))
    up = jnp.where(rows == ROWS - 1, 0.0, pltpu.roll(v, ROWS - 1, 0))
    return down + up + pltpu.roll(v, 1, 1) + pltpu.roll(v, lanes - 1, 1)


def doubled(spin_ref, rows):
    return [hund_coupling * spin_ref[i, rows, :] for i in range(3)]


def copy_all(copies):
    for copy in copies:
        copy.start()
    for copy in copies:
        copy.wait()


def y_rows(refs, rows, out, sems, first):
    return [
        pltpu.make_async_copy(
            ref.at[:, :, :, row, :], out.at[j, k], sems.at[first + 2 * j + k]
        )
        for j, row in enumerate(rows)
        for k, ref in enumerate(refs)
    ]


def x_planes(refs, planes, outs, sems, first):
    return [
        pltpu.make_async_copy(
            ref.at[:, :, plane, :, :], out.at[k], sems.at[first + 2 * j + k]
        )
        for j, (plane, out) in enumerate(zip(planes, outs))
        for k, ref in enumerate(refs)
    ]


def pack_y_kernel(p_ref, l_ref, ysend_ref, sems):
    copy_all(y_rows((p_ref, l_ref), (0, ROWS - 1), ysend_ref, sems, 0))


def pack_x_kernel(p_ref, l_ref, xlo_ref, xhi_ref, sems):
    wide = p_ref.shape[2]
    copy_all(x_planes((p_ref, l_ref), (0, wide - 1), (xlo_ref, xhi_ref), sems, 0))


def inner_kernel(
    s_ref, p_hbm, l_hbm, s_hbm, n_hbm,
    g_ref, fx_ref, fy_ref, xin_ref, yin_ref, sy_ref, ny_ref,
    p_ref, l_ref, f_ref, a_ref, sems, field_sems,
):
    probes, _, wide = p_ref.shape[:3]
    half = f_ref.shape[3]

    def fetch(q):
        return [
            pltpu.make_async_copy(src.at[:, q], dst.at[q], field_sems.at[k, q])
            for k, (src, dst) in enumerate(((p_hbm, p_ref), (l_hbm, l_ref)))
        ]

    for q in range(probes):
        for copy in fetch(q):
            copy.start()
    copies = x_planes((p_hbm, l_hbm), (1, wide - 2), (xin_ref.at[0], xin_ref.at[1]), sems, 0)
    copies += y_rows((p_hbm, l_hbm), (1, ROWS - 2), yin_ref, sems, 4)
    copies += [
        pltpu.make_async_copy(src.at[:, :, row, :], dst.at[j], sems.at[8 + 2 * k + j])
        for k, (src, dst) in enumerate(((s_hbm, sy_ref), (n_hbm, ny_ref)))
        for j, row in enumerate((0, ROWS - 1))
    ]
    for copy in copies:
        copy.start()
    g_ref[...] = jnp.zeros_like(g_ref)

    def at(x):
        return slice(x * ROWS, (x + 1) * ROWS)

    def joined(ref):
        return lambda c, x: jnp.concatenate([ref[c, 0, at(x), :], ref[c, 1, at(x), :]], 1)

    def neighbours(load, c, x, centre):
        total = along(centre)
        if x > 0:
            total = total + load(c, x - 1)
        if x < wide - 1:
            total = total + load(c, x + 1)
        return total

    @pl.loop(0, probes)
    def _(q):
        for copy in fetch(q):
            copy.wait()

        def plain(ref):
            return lambda c, x: ref[q, c, x]

        load_p, load_l, load_f, load_a = plain(p_ref), plain(l_ref), joined(f_ref), joined(a_ref)
        for x in range(wide):
            spin = doubled(s_ref, at(x))
            for load, dst, extra in ((load_p, f_ref, 0.0), (load_l, a_ref, lift)):
                v = [load(c, x) for c in range(4)]
                m = onsite(spin, v)
                for c in range(4):
                    out = neighbours(load, c, x, v[c]) + m[c]
                    if extra:
                        out = out + extra * v[c]
                    dst[c, 0, at(x), :] = out[:, :half]
                    dst[c, 1, at(x), :] = out[:, half:]
        for x in range(wide):
            spin = doubled(s_ref, at(x))
            p, l, f, a = (
                [load(c, x) for c in range(4)] for load in (load_p, load_l, load_f, load_a)
            )
            ma, mf = onsite(spin, a), onsite(spin, f)
            ha = [neighbours(load_a, c, x, a[c]) + ma[c] - tilt * l[c] for c in range(4)]
            hf = [neighbours(load_f, c, x, f[c]) + mf[c] for c in range(4)]
            total = plus(bilinear(ha, p), bilinear(a, f), bilinear(l, hf))
            for i in range(3):
                g_ref[i, at(x), :] += total[i]
        for k, ref in enumerate((f_ref, a_ref)):
            for c in range(4):
                for z in range(2):
                    lanes = slice(z * half, (z + 1) * half)
                    fx_ref[0, k, c, q, :, lanes] = ref[c, z, at(0), :]
                    fx_ref[1, k, c, q, :, lanes] = ref[c, z, at(wide - 1), :]
                    fy_ref[0, k, c, q, :, lanes] = ref[c, z, pl.ds(0, wide, stride=ROWS), :]
                    fy_ref[1, k, c, q, :, lanes] = ref[
                        c, z, pl.ds(ROWS - 1, wide, stride=ROWS), :
                    ]

    for copy in copies:
        copy.wait()


def own_change(spin, p, l, p_in, l_in, f, a, dp, dl):
    hp = plus(onsite(spin, dp), [along(v) for v in dp])
    hl = plus(onsite(spin, dl), [along(v) for v in dl])
    here = plus(
        bilinear(dl, plus(f, dp)), bilinear(a, dp), bilinear(hl, p), bilinear(l, hp)
    )
    inward = plus(bilinear(dl, p_in), bilinear(l_in, dp))
    return here, inward


def corner_rows(lo_ref, hi_ref, k, c, row, wide, lanes):
    rows = lax.broadcasted_iota(jnp.int32, (wide, lanes), 0)
    low = jnp.broadcast_to(lo_ref[k, c, row : row + 1, :], (wide, lanes))
    high = jnp.broadcast_to(hi_ref[k, c, row : row + 1, :], (wide, lanes))
    return jnp.where(rows == 0, low, jnp.where(rows == wide - 1, high, 0.0))


def over_probes(probes, body, results, like, unroll):
    zero = jnp.zeros(like, F32)
    return lax.fori_loop(0, probes, body, (zero,) * results, unroll=unroll)


def spinors(ref, k, q):
    return [ref[k, c, q] for c in range(4)]


def message(f, a, dp, dl):
    return plus(bilinear(plus(a, dl), dp), bilinear(dl, plus(f, dp)))


def x_message_kernel(fx_ref, lo_ref, hi_ref, mlo_ref, mhi_ref):
    probes = fx_ref.shape[3]
    for side, halo, out in ((0, lo_ref, mlo_ref), (1, hi_ref, mhi_ref)):

        def body(q, total):
            f, a = (spinors(fx_ref.at[side], k, q) for k in range(2))
            dp, dl = (spinors(halo, k, q) for k in range(2))
            return tuple(plus(total, message(f, a, dp, dl)))

        total = over_probes(probes, body, 3, out.shape[1:], 2)
        for i in range(3):
            out[i] = total[i]


def x_kernel(
    fx_ref, fy_ref, lo_ref, hi_ref, xlo_ref, xhi_ref, xin_ref, s_ref, gx_ref, fc_ref, fe_ref
):
    probes = fx_ref.shape[3]
    wide, lanes = fy_ref.shape[4:]
    for side, halo, edge, x in ((0, lo_ref, xlo_ref, 0), (1, hi_ref, xhi_ref, wide - 1)):
        spin = doubled(s_ref, slice(x * ROWS, (x + 1) * ROWS))

        def body(q, total):
            f, a = (spinors(fx_ref.at[side], k, q) for k in range(2))
            dp, dl = (spinors(halo, k, q) for k in range(2))
            p, l = (spinors(edge, k, q) for k in range(2))
            p_in, l_in = (spinors(xin_ref.at[side], k, q) for k in range(2))
            here, inward = own_change(spin, p, l, p_in, l_in, f, a, dp, dl)
            row = side * (ROWS - 1)
            for k in range(2):
                for c in range(4):
                    t = corner_rows(lo_ref.at[:, :, q], hi_ref.at[:, :, q], k, c, row, wide, lanes)
                    once = fy_ref[side, k, c, q] + t
                    fc_ref[side, k, c, q] = once
                    fe_ref[side, k, c, q] = once + t
            return tuple(plus(total, here + inward))

        total = over_probes(probes, body, 6, (ROWS, lanes), 1)
        for j in range(2):
            for i in range(3):
                gx_ref[side, j, i] = total[3 * j + i]


def y_message_kernel(recv_ref, fe_ref, base_ref, my_ref):
    probes = fe_ref.shape[3]
    for side in range(2):

        def body(q, total):
            f, a = (spinors(fe_ref.at[side], k, q) for k in range(2))
            dp, dl = (spinors(recv_ref.at[1 - side], k, q) for k in range(2))
            return tuple(plus(total, message(f, a, dp, dl)))

        total = over_probes(probes, body, 3, my_ref.shape[2:], 2)
        for i in range(3):
            my_ref[side, i] = total[i]


def y_kernel(recv_ref, ysend_ref, yin_ref, fc_ref, sy_ref, gy_ref):
    probes = fc_ref.shape[3]
    wide, lanes = fc_ref.shape[4:]
    for side in range(2):
        spin = [hund_coupling * sy_ref[side, i] for i in range(3)]

        def body(q, total):
            dp, dl = (spinors(recv_ref.at[1 - side], k, q) for k in range(2))
            f, a = (spinors(fc_ref.at[side], k, q) for k in range(2))
            p, l = (spinors(ysend_ref.at[side], k, q) for k in range(2))
            p_in, l_in = (spinors(yin_ref.at[side], k, q) for k in range(2))
            here, inward = own_change(spin, p, l, p_in, l_in, f, a, dp, dl)
            return tuple(plus(total, here + inward))

        total = over_probes(probes, body, 6, (wide, lanes), 1)
        for j in range(2):
            for i in range(3):
                gy_ref[side, j, i] = total[3 * j + i]


def cross(a, b):
    return [
        a[1] * b[2] - a[2] * b[1],
        a[2] * b[0] - a[0] * b[2],
        a[0] * b[1] - a[1] * b[0],
    ]


def base_kernel(g_ref, gx_ref, mlo_ref, mhi_ref, base_ref):
    wide = g_ref.shape[1] // ROWS
    half = base_ref.shape[3]
    for x in range(wide):
        here = slice(x * ROWS, (x + 1) * ROWS)
        for i in range(3):
            g = g_ref[i, here, :]
            for side, edge, step, m_ref in ((0, 0, 1, mlo_ref), (1, wide - 1, -1, mhi_ref)):
                if x == edge:
                    g = g + gx_ref[side, 0, i] + m_ref[i]
                if x == edge + step:
                    g = g + gx_ref[side, 1, i]
            for z in range(2):
                base_ref[i, z, here, :] = g[:, z * half : (z + 1) * half]


def turn(s, field):
    torque = cross(s, field)
    twist = cross(s, torque)
    return [-time_step * t - time_step * damping * w for t, w in zip(torque, twist)]


def stepped(s, field, noise):
    kick = cross(s, noise)
    return [a + b + kick_scale * c for a, b, c in zip(s, turn(s, field), kick)]


def finish_kernel(scale, g_ref, gy_ref, s_ref, n_ref, sy_ref, ny_ref, o_ref, r_ref):
    wide, lanes = gy_ref.shape[3:]
    rows = lax.broadcasted_iota(jnp.int32, (ROWS, lanes), 0)

    def joined(i, where):
        return jnp.concatenate([g_ref[i, 0, where, :], g_ref[i, 1, where, :]], 1)

    for side, row in ((0, 0), (1, ROWS - 1)):
        field = [
            scale * (joined(i, pl.ds(row, wide, stride=ROWS)) + gy_ref[side, 0, i])
            for i in range(3)
        ]
        s, n = ([ref[side, i] for i in range(3)] for ref in (sy_ref, ny_ref))
        for i, value in enumerate(stepped(s, field, n)):
            r_ref[side, i] = value
    for x in range(wide):
        here = slice(x * ROWS, (x + 1) * ROWS)
        field = []
        for i in range(3):
            low, high = (
                jnp.broadcast_to(gy_ref[side, 1, i, x : x + 1, :], (ROWS, lanes))
                for side in range(2)
            )
            inner = jnp.where(rows == 1, low, jnp.where(rows == ROWS - 2, high, 0.0))
            field.append(scale * (joined(i, here) + inner))
        s, n = ([ref[i, here, :] for i in range(3)] for ref in (s_ref, n_ref))
        for i, value in enumerate(stepped(s, field, n)):
            o_ref[i, x] = value


def final_kernel(scale, whole_ref, r_ref, my_ref, sy_ref, o_ref, rows_ref, sems):
    for side in range(2):
        field = [scale * my_ref[1 - side, i] for i in range(3)]
        change = turn([sy_ref[side, i] for i in range(3)], field)
        for i in range(3):
            rows_ref[side, i] = r_ref[side, i] + change[i]
    copy_all(
        [
            pltpu.make_async_copy(rows_ref.at[j], o_ref.at[:, :, row, :], sems.at[j])
            for j, row in enumerate((0, ROWS - 1))
        ]
    )


def call(kernel, name, out_shape, flops, moved, **kw):
    limit = kw.pop("limit", 16)
    return pl.pallas_call(
        kernel,
        out_shape=[jax.ShapeDtypeStruct(s, F32) for s in out_shape],
        compiler_params=pltpu.CompilerParams(vmem_limit_bytes=limit * MIB),
        cost_estimate=pl.CostEstimate(flops=flops, bytes_accessed=moved, transcendentals=0),
        name=name,
        **kw,
    )


def local(spins, probes, left_probes, noise):
    _, count, wide, tall, deep = probes.shape
    assert tall == ROWS and wide == ROWS
    sites = wide * tall
    p5, l5, s4, n4 = (
        pltpu.with_memory_space_constraint(v, pltpu.HBM)
        for v in (probes, left_probes, spins, noise)
    )
    s, n = spins.reshape(3, sites, deep), noise.reshape(3, sites, deep)
    volume = 4 * count * sites * deep
    plane = (4, count, ROWS, deep)
    pair = (2, 2) + plane
    vmem = pl.BlockSpec(memory_space=pltpu.VMEM)
    hbm = pl.BlockSpec(memory_space=pltpu.HBM)

    def meet(both):
        if lax.axis_size("gy") == 2:
            return shifted(both, "gy", 1)
        return jnp.stack([shifted(both[0], "gy", -1), shifted(both[1], "gy", 1)])

    (ysend,) = call(
        pack_y_kernel, "pack_y", [pair], volume, 2 * volume,
        in_specs=[hbm] * 2, out_specs=[vmem],
        scratch_shapes=[pltpu.SemaphoreType.DMA((4,))],
    )(p5, l5)
    recv = meet(ysend)
    xlo, xhi = call(
        pack_x_kernel, "pack_x", [(2,) + plane] * 2, volume, 2 * volume,
        in_specs=[hbm] * 2, out_specs=[vmem] * 2,
        scratch_shapes=[pltpu.SemaphoreType.DMA((4,))],
    )(p5, l5)
    hi = shifted(xlo, "gx", -1)
    lo = shifted(xhi, "gx", 1)

    rows = (2, 3, wide, deep)
    g, fx, fy, xin, yin, sy, ny = call(
        inner_kernel, "inner", [(3, sites, deep)] + [pair] * 4 + [rows] * 2,
        80 * volume, 16 * volume,
        in_specs=[vmem] + [hbm] * 4, out_specs=[vmem] * 7,
        scratch_shapes=[pltpu.VMEM((count, 4, wide, ROWS, deep), F32)] * 2
        + [pltpu.VMEM((4, 2, sites, deep // 2), F32)] * 2
        + [pltpu.SemaphoreType.DMA((12,)), pltpu.SemaphoreType.DMA((2, count))],
    )(s, p5, l5, s4, n4)

    mlo, mhi = call(
        x_message_kernel, "message_x", [(3, ROWS, deep)] * 2, 5 * volume, 4 * volume,
        in_specs=[vmem] * 3, out_specs=[vmem] * 2,
    )(fx, lo, hi)
    mhi_recv = shifted(mlo, "gx", -1)
    mlo_recv = shifted(mhi, "gx", 1)
    gx, fc, fe = call(
        x_kernel, "edges_x", [(2, 2, 3, ROWS, deep), pair, pair], 20 * volume, 8 * volume,
        in_specs=[vmem] * 8, out_specs=[vmem] * 3,
    )(fx, fy, lo, hi, xlo, xhi, xin, s)
    (base,) = call(
        base_kernel, "base", [(3, 2, sites, deep // 2)], volume, volume,
        in_specs=[vmem] * 4, out_specs=[vmem],
    )(g, gx, mlo_recv, mhi_recv)

    (my,) = call(
        y_message_kernel, "message_y", [(2, 3, wide, deep)], 5 * volume, 4 * volume,
        in_specs=[vmem] * 2 + [pl.BlockSpec(memory_space=pl.ANY)], out_specs=[vmem],
    )(recv, fe, base)
    my_recv = meet(my)
    (gy,) = call(
        y_kernel, "edges_y", [(2, 2, 3, wide, deep)], 20 * volume, 8 * volume,
        in_specs=[vmem] * 5, out_specs=[vmem],
    )(recv, ysend, yin, fc, sy)

    scale = hund_coupling / spread / count * unit
    early, edge_rows = call(
        functools.partial(finish_kernel, scale), "finish", [spins.shape, rows],
        volume, volume, in_specs=[vmem] * 6, out_specs=[vmem] * 2,
    )(base, gy, s, n, sy, ny)
    (out,) = call(
        functools.partial(final_kernel, scale), "final", [spins.shape], volume // 8, volume // 8,
        in_specs=[hbm] + [vmem] * 3, out_specs=[hbm], input_output_aliases={0: 0},
        scratch_shapes=[pltpu.VMEM(rows, F32), pltpu.SemaphoreType.DMA((2,))],
    )(early, edge_rows, my_recv, sy)
    return out


def solution(mesh):
    placed = (
        P(None, "gx", "gy", None),
        P(None, None, "gx", "gy", None),
        P(None, None, "gx", "gy", None),
        P(None, "gx", "gy", None),
    )
    return jax.shard_map(
        local, mesh=mesh, in_specs=placed, out_specs=P(None, "gx", "gy", None), check_vma=False
    )
```
